512 devices in a mesh: group: 8 (over x, z_lo), shard: 64 (over z_hi, y, core).
Axes of the slice: x: 4, y: 8, z: 8 (z_hi: 4, z_lo: 2; z = z_hi * 2 + z_lo), core: 2. Of those that a mesh axis runs over, the one named last changes fastest.
Arguments:
- tokens: bfloat16 [512, 3072], P('group', 'shard'), may hold values from -6 to 6
- cotangent: bfloat16 [512, 3072], P('group', 'shard'), may hold values from -1.5 to 1.5
- expert_ids: int32 [512, 2], P('group'), may hold values from 0 to 7, all different within a row; in each aligned block of 64 rows (0 to 63, 64 to 127, ...) at most 36 rows name the same one
- route_weight: float32 [512, 2], P('group'), may hold values from 0.1 to 0.9
- w_gate: bfloat16 [8, 3072, 8192], P('group', None, 'shard'), may hold values from -0.109375 to 0.109375
- w_up: bfloat16 [8, 3072, 8192], P('group', None, 'shard'), may hold values from -0.109375 to 0.109375
- w_down: bfloat16 [8, 8192, 3072], P('group', 'shard'), may hold values from -0.109375 to 0.109375
Outputs:
- grad_tokens: bfloat16 [512, 3072], P('group', 'shard')
- grad_gate: bfloat16 [8, 3072, 8192], P('group', None, 'shard')
- grad_up: bfloat16 [8, 3072, 8192], P('group', None, 'shard')
The draws below stay inside these ranges and needn't reach their ends.
Inputs may be any that keep to these rules, and one draw needn't show every extreme that they name: `expert_ids`: each token names 2 different experts. Among the 64 tokens of one aligned block (the tokens of one index of group), no expert is named by more than 36 tokens.
All inputs are finite; a program needn't handle non-finite values.
Results may differ from the reference program's by a relative error of at most 0.0064.
Values may be sent and summed in bfloat16 or wider, within the bound.
A program may use at most 64 MiB of HBM per device.

```python
import math
import jax
import jax.numpy as jnp
import numpy as np
from jax import lax

D = 3072
FF = 8192
EXPERTS = 8
TOPK = 2
TOK_GRP = 64
CAP = 36
TOKENS = 512
N_GROUP = 8


def block_scale(stream_key, extent, split, low, largest):
    factor_of, own = 1.0, jax.random.fold_in(stream_key, 6)
    for position, parts in split:
        heights = jnp.exp(jax.random.uniform(jax.random.fold_in(own, position), (parts,), jnp.float32, low / len(split), largest / len(split)))
        factor_of = factor_of * jnp.repeat(heights, extent[position] // parts).reshape([-1 if axis == position else 1 for axis in range(len(extent))])
    return factor_of


def routed_block(rng, own, number, rows, number_of, top, limit, skew):
    order = jax.random.permutation(rng, number_of)
    crowded, common = shares(number_of, rows * top, limit, skew, True), shares(number_of, rows * top, limit, skew, False)
    places = jnp.arange(number_of)

    def named(lengths, turn):
        used = int((lengths > 0).sum())
        fixed = max(1, used // 4)
        passed = fixed + (places - fixed + turn * (used - fixed)) % max(1, number_of - fixed)
        return jnp.zeros((number_of,), jnp.int32).at[order[jnp.where(places < fixed, places, passed)]].set(jnp.asarray(lengths, jnp.int32))

    lengths = jnp.where(number % 4 == 0, named(crowded, number // 4), named(common, number - number // 4 - 1))
    mixed = jax.random.permutation(jax.random.fold_in(own, 3), number_of)
    donor, taker = mixed[0:number_of // 2 * 2:2], mixed[1:number_of // 2 * 2:2]
    margin = jnp.minimum(lengths[donor] - 1, limit - lengths[taker]) // 2
    margin = jnp.where((donor == order[0]) | (taker == order[0]) | (lengths[taker] == 0), 0, jnp.maximum(margin, 0))
    passed = jax.random.randint(jax.random.fold_in(own, 4), (number_of // 2,), 0, 1 << 20) % (margin + 1)
    lengths = lengths.at[donor].add(-passed).at[taker].add(passed)
    members = jnp.searchsorted(jnp.cumsum(lengths), jnp.arange(rows * top), side="right").astype(jnp.int32)
    listing = members.reshape(top, rows).T
    listing = listing[jax.random.permutation(jax.random.fold_in(own, 1), rows)]
    turn = jax.random.randint(jax.random.fold_in(own, 2), (rows, 1), 0, top)
    return jnp.take_along_axis(listing, (jnp.arange(top)[None, :] + turn) % top, axis=1)


def shares(number_of, total, bound, lean, full):
    loads = [(1 << 20) // math.isqrt(rank ** lean) + 1 for rank in range(1, number_of + 1)]
    largest = bound if full else min(bound, max(-(-total // number_of), total * loads[0] // sum(loads)))
    least = 1 if total - largest >= number_of - 1 else 0
    counts, rest = [largest] + [least] * (number_of - 1), total - largest - least * (number_of - 1)
    while rest > 0:
        movable = [i for i in range(1, number_of) if counts[i] < largest] or [i for i in range(1, number_of) if counts[i] < bound]
        pool, remaining = sum([loads[i] for i in movable]), rest
        for i in movable:
            more = min(bound - counts[i], max(1, remaining * loads[i] // pool), rest)
            counts[i] = counts[i] + more
            rest = rest - more
    return np.array(counts)


def bell_draw(own_key, shape, width, limit, pieces=(), kind=jnp.bfloat16):
    entries = jax.random.normal(own_key, shape, jnp.float32) * width
    if len(pieces) > 0:
        entries = block_scale(own_key, shape, pieces, -0.22, 0.18) * entries
    return jnp.clip(entries, min=-limit, max=limit).astype(kind)


def setup_inputs(seed: int = 0) -> dict:
    key_list = jax.random.split(jax.random.key(seed), 8)
    tokens = bell_draw(key_list[0], (TOKENS, D), 1.0, 6.0, ((0, 8), (1, 64)))
    cotangent = bell_draw(key_list[1], (TOKENS, D), 0.25, 1.5, ((0, 8), (1, 64)))
    expert_ids_keys = jax.random.split(jax.random.fold_in(key_list[2], 1), TOKENS // TOK_GRP)
    expert_ids_turns = jax.random.permutation(jax.random.fold_in(key_list[2], 3), TOKENS // TOK_GRP)
    expert_ids = jax.vmap(lambda own, number: routed_block(jax.random.fold_in(key_list[2], 2), own, number, TOK_GRP, EXPERTS, TOPK, CAP, 2))(expert_ids_keys, expert_ids_turns).reshape((TOKENS, TOPK))
    route_weight = jnp.clip(0.1 + 0.79999997 * jax.random.uniform(key_list[3], (TOKENS, TOPK), jnp.float32) ** block_scale(key_list[3], (TOKENS, TOPK), ((0, 8),), -0.2, 0.2), 0.1, 0.9)
    w_gate = bell_draw(key_list[4], (EXPERTS, D, FF), D ** -0.5, 0.109375, ((0, 8), (2, 64)))
    w_up = bell_draw(key_list[5], (EXPERTS, D, FF), D ** -0.5, 0.109375, ((0, 8), (2, 64)))
    w_down = bell_draw(key_list[6], (EXPERTS, FF, D), D ** -0.5, 0.109375, ((0, 8), (1, 64)))
    return dict(tokens=tokens, cotangent=cotangent, expert_ids=expert_ids, route_weight=route_weight, w_gate=w_gate, w_up=w_up, w_down=w_down)


exact_mode = lax.Precision.HIGHEST


def slot_table(expert_ids, capacity):
    experts_axis = jnp.arange(EXPERTS, dtype=jnp.int32)
    counted = jnp.sum((expert_ids[:, :, None] == experts_axis[None, None, :]).astype(jnp.int32), axis=1)
    ranking = jnp.cumsum(counted, axis=0).astype(jnp.int32) - 1
    places = jnp.arange(capacity, dtype=jnp.int32)
    slot_map = (counted.T[:, None, :] == 1) & (ranking.T[:, None, :] == places[None, :, None])
    return counted, slot_map


def slot_scales(slot_map, expert_ids, route_weight):
    experts_axis = jnp.arange(EXPERTS, dtype=jnp.int32)
    per_expert = jnp.sum(jnp.where(expert_ids[:, :, None] == experts_axis[None, None, :], route_weight[:, :, None], jnp.float32(0.0)), axis=1)
    return jnp.einsum("ect,te->ec", slot_map.astype(jnp.float32), per_expert, precision=exact_mode)


def slot_grads(slot_inputs, slot_cotangents, paired, down_weight):
    hidden_width = down_weight.shape[0]
    joined = jnp.dot(slot_inputs, paired, preferred_element_type=jnp.float32)
    gate_pre = joined[:, :hidden_width]
    up_value = joined[:, hidden_width:]
    sigmoid_gate = jax.nn.sigmoid(gate_pre)
    active = gate_pre * sigmoid_gate
    hidden_grad = lax.dot_general(slot_cotangents, down_weight, (((1,), (1,)), ((), ())), preferred_element_type=jnp.float32)
    gate_grad = (hidden_grad * up_value * sigmoid_gate * (1.0 + gate_pre * (1.0 - sigmoid_gate))).astype(jnp.bfloat16)
    up_grad = (hidden_grad * active).astype(jnp.bfloat16)
    stacked = jnp.concatenate([gate_grad, up_grad], axis=1)
    input_grad = lax.dot_general(stacked, paired, (((1,), (1,)), ((), ())), preferred_element_type=jnp.float32)
    return input_grad, stacked


def source_partials(slot_inputs, stacked, sources):
    capacity = slot_inputs.shape[0] // sources

    def accumulate(source, running):
        begin = (source * capacity).astype(jnp.int32)
        piece_inputs = lax.dynamic_slice_in_dim(slot_inputs, begin, capacity, 0)
        piece_grads = lax.dynamic_slice_in_dim(stacked, begin, capacity, 0)
        partial_sum = lax.dot_general(piece_inputs, piece_grads, (((0,), (0,)), ((), ())), preferred_element_type=jnp.float32)
        return running + lax.optimization_barrier(partial_sum.astype(jnp.bfloat16)).astype(jnp.float32)

    initial = jnp.zeros((slot_inputs.shape[1], stacked.shape[1]), jnp.float32)
    return lax.fori_loop(jnp.int32(0), jnp.int32(sources), accumulate, initial)


def reference(tokens, cotangent, expert_ids, route_weight, w_gate, w_up, w_down):
    by_group = tokens.reshape(N_GROUP, TOK_GRP, D).astype(jnp.float32)
    cot_group = cotangent.reshape(N_GROUP, TOK_GRP, D).astype(jnp.float32)
    ids_group = expert_ids.reshape(N_GROUP, TOK_GRP, TOPK)
    weights_group = route_weight.reshape(N_GROUP, TOK_GRP, TOPK)
    tables = []
    scale_list = []
    for group_id in range(N_GROUP):
        counted, slot_map = slot_table(ids_group[group_id], CAP)
        tables.append(slot_map)
        scale_list.append(slot_scales(slot_map, ids_group[group_id], weights_group[group_id]))
    table_all = jnp.stack(tables)
    scale_all = jnp.stack(scale_list)
    grad_total = jnp.zeros((N_GROUP, TOK_GRP, D), jnp.float32)
    gate_grads = []
    up_grads = []
    for expert in range(EXPERTS):
        chosen = table_all[:, expert].astype(jnp.float32)
        slot_inputs = jnp.einsum("gct,gtd->gcd", chosen, by_group, precision=exact_mode).astype(jnp.bfloat16).reshape(N_GROUP * CAP, D)
        picked = jnp.einsum("gct,gtd->gcd", chosen, cot_group, precision=exact_mode)
        slot_cotangents = (scale_all[:, expert][:, :, None] * picked).astype(jnp.bfloat16).reshape(N_GROUP * CAP, D)
        paired = jnp.concatenate([w_gate[expert], w_up[expert]], axis=1)
        input_grad, stacked = slot_grads(slot_inputs, slot_cotangents, paired, w_down[expert])
        grad_total = grad_total + jnp.einsum("gct,gcd->gtd", chosen, input_grad.reshape(N_GROUP, CAP, D), precision=exact_mode)
        running = source_partials(slot_inputs, stacked, N_GROUP)
        gate_grads.append(running[:, :FF].astype(jnp.bfloat16))
        up_grads.append(running[:, FF:].astype(jnp.bfloat16))
    return grad_total.reshape(TOKENS, D).astype(jnp.bfloat16), jnp.stack(gate_grads), jnp.stack(up_grads)
```

```python
import functools

import jax
import jax.numpy as jnp
from jax import lax
from jax.experimental import pallas as pl
from jax.experimental.pallas import tpu as pltpu
from jax.sharding import PartitionSpec as P

CAP = 36
LANES = 128
TOK_LANES = 384
ALL_LANES = 640
BF, F32 = jnp.bfloat16, jnp.float32
MESH = pl.DeviceIdType.MESH


def nt(a, b):
    return lax.dot_general(a, b, (((1,), (1,)), ((), ())), preferred_element_type=F32)


def nn(a, b):
    return lax.dot_general(a, b, (((1,), (0,)), ((), ())), preferred_element_type=F32)


def iota(shape, dim):
    return lax.broadcasted_iota(jnp.int32, shape, dim)


def kernel(
    dims, tok, cot, ids, wts, wg_hbm, wu_hbm, wd_hbm, out, gg_hbm, gu_hbm,
    wg, wu, wd, wt, picks, sent, got, spread, gath, dx, pair, ring_in, ring_out,
    zsum_out, zsum_in, pull, back, home, gbuf, ubuf, lsem, gsend, grecv, zsend, zrecv,
    ysend, yrecv, csend, crecv, psend, precv, rsend, rrecv, wsend, wrecv, hsend, hrecv,
):
    NG, ZH, NY, feat, toks = dims
    rows = feat * 2 * NY
    g = lax.axis_index("group")
    s = lax.axis_index("shard")
    c = lax.rem(s, 2)
    y = lax.rem(lax.div(s, 2), NY)
    z = lax.div(s, 2 * NY)

    def shard_id(zz, yy, cc):
        return (zz * NY + yy) * 2 + cc

    def wrap(v, n):
        return lax.rem(v + 2 * n, n)

    other = shard_id(z, y, 1 - c)
    right = shard_id(z, wrap(y + 1, NY), c)
    left = shard_id(z, wrap(y - 1, NY), c)

    barrier = pltpu.get_barrier_semaphore()

    def greet(gg, ss):
        pl.semaphore_signal(barrier, inc=1, device_id={"group": gg, "shard": ss}, device_id_type=MESH)

    for k in range(1, NG):
        greet(wrap(g + k, NG), s)
    for k in range(1, ZH):
        greet(g, shard_id(wrap(z + k, ZH), y, c))
    greet(g, right)
    greet(g, left)
    greet(g, other)

    loads = [
        pltpu.make_async_copy(h.at[0], v, lsem.at[i])
        for i, (h, v) in enumerate(((wg_hbm, wg), (wu_hbm, wu), (wd_hbm, wd)))
    ]
    for copy in loads:
        copy.start()

    def send(src, dst, ssem, rsem, gg, ss):
        copy = pltpu.make_async_remote_copy(
            src_ref=src, dst_ref=dst, send_sem=ssem, recv_sem=rsem,
            device_id={"group": gg, "shard": ss}, device_id_type=MESH,
        )
        copy.start()
        pending.append(copy)

    def arrived(dst, ssem, rsem, gg, ss):
        pltpu.make_async_remote_copy(
            src_ref=dst, dst_ref=dst, send_sem=ssem, recv_sem=rsem,
            device_id={"group": gg, "shard": ss}, device_id_type=MESH,
        ).wait_recv()

    pending = []

    who = iota((16, toks), 0)
    first, second = ids[0:1, :] == who, ids[1:2, :] == who
    hit = jnp.where(first, 1, 0) + jnp.where(second, 1, 0)
    upto = jnp.where(iota((toks, toks), 0) <= iota((toks, toks), 1), 1.0, 0.0).astype(BF)
    rank = nn(hit.astype(F32).astype(BF), upto).astype(jnp.int32) - 1
    rank = jnp.where((hit == 1) & (rank < CAP), rank, -1000)
    scale = jnp.where(first, wts[0:1, :], 0.0) + jnp.where(second, wts[1:2, :], 0.0)
    slot = iota((LANES, toks), 0)
    tok_b = tok[...]
    cot_f = cot[...].astype(F32)
    for e in range(NG):
        pick = jnp.where(slot == rank[e : e + 1, :], 1.0, 0.0).astype(BF)
        pick_cot = jnp.where(slot == rank[e : e + 1, :] + CAP, 1.0, 0.0).astype(BF)
        scaled = (cot_f * scale[e : e + 1, :]).astype(BF)
        picks[e] = pick
        sent[e] = (nt(tok_b, pick) + nt(scaled, pick_cot)).astype(BF)

    pl.semaphore_wait(barrier, (NG - 1) + (ZH - 1) + 3)

    for k in range(1, NG):
        e = wrap(g + k, NG)
        send(sent.at[e], got.at[g], gsend.at[k], grecv.at[NG - k], e, s)

    lane = iota((LANES, 1), 0)
    for e in range(NG):
        j = lane + CAP * e
        jc = j - CAP
        to = jnp.where(lane < CAP, j, jnp.where(jc < 256, jc + TOK_LANES, jc + 32))
        to = jnp.where(lane < 2 * CAP, to, -1)
        spread[e] = jnp.where(iota((LANES, ALL_LANES), 1) == to, 1.0, 0.0).astype(BF)
    got[g] = sent[g]
    for k in range(1, NG):
        e = wrap(g - k, NG)
        arrived(got.at[e], gsend.at[k], grecv.at[k], e, s)
    block = nn(got[0], spread[0])
    for e in range(1, NG):
        block = block + nn(got[e], spread[e])
    mine = pl.multiple_of(s * feat, 16)
    gath[pl.ds(mine, feat), :] = block.astype(BF)

    def place(zz, yy, cc):
        return gath.at[pl.ds(pl.multiple_of(shard_id(zz, yy, cc) * feat, 16), feat), :]

    reach = [[NY // 2, NY - 1 - NY // 2] if k % 2 == 0 else [NY - 1 - NY // 2, NY // 2] for k in range(ZH)]

    def pass_on(k, direction, t):
        step = 1 if direction == 0 else -1
        if t < reach[k][direction]:
            at = place(wrap(z + k, ZH), wrap(y - step * t, NY), c)
            send(at, at, ysend.at[k, direction, t], yrecv.at[k, direction, t], g, right if direction == 0 else left)

    def across(k, j):
        at = place(wrap(z + k, ZH), wrap(y + j, NY), c)
        send(at, at, csend.at[k, j], crecv.at[k, j], g, other)

    pass_on(0, 0, 0)
    pass_on(0, 1, 0)
    at = place(z, y, c)
    for k in range(1, ZH):
        to = shard_id(wrap(z + k, ZH), y, c)
        send(at, at, zsend.at[k], zrecv.at[ZH - k], g, to)
    across(0, 0)

    for copy in loads:
        copy.wait()
    eye = jnp.where(iota((LANES, LANES), 0) == iota((LANES, LANES), 1), 1.0, 0.0).astype(BF)
    depth = wg.shape[0]
    part = depth // 4
    for i in range(4):
        cols = slice(i * part, (i + 1) * part)
        wt[0:LANES, cols] = nt(eye, wg[cols, :]).astype(BF)
        wt[LANES : 2 * LANES, cols] = nt(eye, wu[cols, :]).astype(BF)

    order = [0] + [k for k in (1, ZH - 1) if 0 < k < ZH] + [2]
    order = list(dict.fromkeys(k for k in order if k < ZH))
    lag = {k: 0 if k == 0 else 1 for k in order}
    far = max(max(r) for r in reach)
    for wave in range(1, far + 2):
        for k in order:
            t = wave - lag[k]
            if t == 0 and k > 0:
                src = shard_id(wrap(z + k, ZH), y, c)
                arrived(place(wrap(z + k, ZH), y, c), zsend.at[k], zrecv.at[k], g, src)
                pass_on(k, 0, 0)
                pass_on(k, 1, 0)
                across(k, 0)
            for direction in (0, 1):
                step = 1 if direction == 0 else -1
                if 1 <= t <= reach[k][direction]:
                    at = place(wrap(z + k, ZH), wrap(y - step * t, NY), c)
                    arrived(at, ysend.at[k, direction, t - 1], yrecv.at[k, direction, t - 1], g, left if direction == 0 else right)
                    pass_on(k, direction, t)
                    across(k, (-step * t) % NY)
    for k in range(ZH):
        for j in range(NY):
            arrived(place(wrap(z + k, ZH), wrap(y + j, NY), 1 - c), csend.at[k, j], crecv.at[k, j], g, other)

    pre = nn(wt[...], gath[:, 0:TOK_LANES])
    hid = nn(wd[...], gath[:, 256:ALL_LANES])
    hid = jnp.concatenate([hid[:, 128:384], pltpu.roll(hid[:, 0:128], 96, 1)], axis=1)
    gate_pre, up_value = pre[0:LANES, :], pre[LANES : 2 * LANES, :]
    sig = 1.0 / (1.0 + jnp.exp(-gate_pre))
    live = iota((LANES, TOK_LANES), 1) < NG * CAP
    gate_grad = jnp.where(live, hid * up_value * sig * (1.0 + gate_pre * (1.0 - sig)), 0.0).astype(BF)
    up_grad = jnp.where(live, hid * gate_pre * sig, 0.0).astype(BF)

    many = 8 if NY % 8 == 0 else NY
    tall = many * feat
    pieces = (ZH * NY * 2) // many
    each = many // 2
    swaps = []
    for i in range(pieces):
        r = slice(i * tall, (i + 1) * tall)
        v = (nn(wg[r, :], gate_grad) + nn(wu[r, :], up_grad)).astype(BF)
        for m in range(each):
            for cc in range(2):
                dx[cc, i * each + m] = v[(2 * m + cc) * feat : (2 * m + cc + 1) * feat, :]
        here = pl.ds(i * each, each)
        send(dx.at[1 - c, here], pair.at[here], psend.at[i], precv.at[i], g, other)
    for i in range(pieces):
        here = pl.ds(i * each, each)
        arrived(pair.at[here], psend.at[i], precv.at[i], g, other)

    def own(k, yy):
        at = wrap(z + k, ZH) * NY + yy
        return dx[c, at].astype(F32) + pair[at].astype(F32)

    stores = []

    def weight_grads(i):
        r = slice(i * tall, (i + 1) * tall)
        x = gath[r, 0:TOK_LANES]
        gbuf[r, :] = nt(x, gate_grad).astype(BF)
        ubuf[r, :] = nt(x, up_grad).astype(BF)

    finish = [k for k in order if k][::-1] + [0]
    done = 0
    for t in range(1, far + 1):
        for k in finish:
            for direction in (0, 1):
                step = 1 if direction == 0 else -1
                length = reach[k][direction]
                if t > length:
                    continue
                v = own(k, wrap(y + step * (length - t + 1), NY))
                if t > 1:
                    at = ring_in.at[k, direction, t - 2]
                    arrived(at, rsend.at[k, direction, t - 2], rrecv.at[k, direction, t - 2], g, left if direction == 0 else right)
                    v = v + at[...].astype(F32)
                ring_out[k, direction, t - 1] = v.astype(BF)
                send(
                    ring_out.at[k, direction, t - 1], ring_in.at[k, direction, t - 1],
                    rsend.at[k, direction, t - 1], rrecv.at[k, direction, t - 1],
                    g, right if direction == 0 else left,
                )
        while done < min(pieces, t * -(-pieces // far)):
            weight_grads(done)
            done += 1
    for buf, hbm, n in ((gbuf, gg_hbm, 3), (ubuf, gu_hbm, 4)):
        copy = pltpu.make_async_copy(buf, hbm.at[0], lsem.at[n])
        copy.start()
        stores.append(copy)
    for e in range(NG):
        j = iota((TOK_LANES, LANES), 0) - CAP * e
        l = iota((TOK_LANES, LANES), 1)
        pull[e] = jnp.where((j == l) & (l < CAP), 1.0, 0.0).astype(BF)
    for k in finish:
        v = own(k, y)
        for direction in (0, 1):
            t = reach[k][direction]
            at = ring_in.at[k, direction, t - 1]
            arrived(at, rsend.at[k, direction, t - 1], rrecv.at[k, direction, t - 1], g, left if direction == 0 else right)
            v = v + at[...].astype(F32)
        if k:
            zsum_out[k] = v.astype(BF)
            to = shard_id(wrap(z + k, ZH), y, c)
            send(zsum_out.at[k], zsum_in.at[ZH - k], wsend.at[k], wrecv.at[ZH - k], g, to)
        else:
            total = v
    for k in range(1, ZH):
        src = shard_id(wrap(z + k, ZH), y, c)
        arrived(zsum_in.at[k], wsend.at[k], wrecv.at[k], g, src)
        total = total + zsum_in[k].astype(F32)
    total = total.astype(BF)

    for e in range(NG):
        back[e] = nn(total, pull[e]).astype(BF)
    for k in range(1, NG):
        e = wrap(g + k, NG)
        send(back.at[e], home.at[g], hsend.at[k], hrecv.at[NG - k], e, s)
    home[g] = back[g]
    for k in range(1, NG):
        e = wrap(g - k, NG)
        arrived(home.at[e], hsend.at[k], hrecv.at[k], e, s)
    res = nn(home[0], picks[0])
    for e in range(1, NG):
        res = res + nn(home[e], picks[e])
    out[...] = res.astype(BF)

    for copy in pending:
        copy.wait_send()
    for copy in stores:
        copy.wait()


def layout(shards):
    ny = 8 if shards == 64 else 4
    return shards // (2 * ny), ny


def body(tokens, cotangent, expert_ids, route_weight, w_gate, w_up, w_down):
    NG, NS = lax.axis_size("group"), lax.axis_size("shard")
    ZH, NY = layout(NS)
    toks, feat = tokens.shape
    depth = NS * feat
    far = NY // 2
    vmem = pl.BlockSpec(memory_space=pltpu.VMEM)
    hbm = pl.BlockSpec(memory_space=pl.ANY)
    dma = pltpu.SemaphoreType.DMA
    half = (ZH * NY, feat, TOK_LANES)
    ring = (ZH, 2, far, feat, TOK_LANES)
    pieces = (ZH * NY * 2) // (8 if NY % 8 == 0 else NY)
    out, gg, gu = pl.pallas_call(
        functools.partial(kernel, (NG, ZH, NY, feat, toks)),
        out_shape=(
            jax.ShapeDtypeStruct((feat, toks), BF),
            jax.ShapeDtypeStruct(w_gate.shape, BF),
            jax.ShapeDtypeStruct(w_up.shape, BF),
        ),
        in_specs=[vmem] * 4 + [hbm] * 3,
        out_specs=(vmem, hbm, hbm),
        scratch_shapes=[
            pltpu.VMEM((depth, LANES), BF),
            pltpu.VMEM((depth, LANES), BF),
            pltpu.VMEM((LANES, depth), BF),
            pltpu.VMEM((2 * LANES, depth), BF),
            pltpu.VMEM((NG, LANES, toks), BF),
            pltpu.VMEM((NG, feat, LANES), BF),
            pltpu.VMEM((NG, feat, LANES), BF),
            pltpu.VMEM((NG, LANES, ALL_LANES), BF),
            pltpu.VMEM((depth, ALL_LANES), BF),
            pltpu.VMEM((2,) + half, BF),
            pltpu.VMEM(half, BF),
            pltpu.VMEM(ring, BF),
            pltpu.VMEM(ring, BF),
            pltpu.VMEM((ZH, feat, TOK_LANES), BF),
            pltpu.VMEM((ZH, feat, TOK_LANES), BF),
            pltpu.VMEM((NG, TOK_LANES, LANES), BF),
            pltpu.VMEM((NG, feat, LANES), BF),
            pltpu.VMEM((NG, feat, LANES), BF),
            pltpu.VMEM((depth, LANES), BF),
            pltpu.VMEM((depth, LANES), BF),
            dma((5,)),
            dma((NG,)), dma((NG,)),
            dma((ZH,)), dma((ZH,)),
            dma((ZH, 2, far)), dma((ZH, 2, far)),
            dma((ZH, NY)), dma((ZH, NY)),
            dma((pieces,)), dma((pieces,)),
            dma((ZH, 2, far)), dma((ZH, 2, far)),
            dma((ZH,)), dma((ZH,)),
            dma((NG,)), dma((NG,)),
        ],
        compiler_params=pltpu.CompilerParams(collective_id=0, has_side_effects=True),
        name="moe_backward",
    )(tokens.T, cotangent.T, expert_ids.T, route_weight.T, w_gate, w_up, w_down)
    return out.T, gg, gu


def solution(mesh):
    in_specs = (
        P("group", "shard"),
        P("group", "shard"),
        P("group", None),
        P("group", None),
        P("group", None, "shard"),
        P("group", None, "shard"),
        P("group", "shard", None),
    )
    out_specs = (P("group", "shard"), P("group", None, "shard"), P("group", None, "shard"))
    return jax.shard_map(body, mesh=mesh, in_specs=in_specs, out_specs=out_specs, check_vma=False)
```

```python
import functools

import jax
import jax.numpy as jnp
from jax import lax
from jax.experimental import pallas as pl
from jax.experimental.pallas import tpu as pltpu
from jax.sharding import PartitionSpec as P

CAP = 36
LANES = 128
TOK_LANES = 384
ALL_LANES = 640
HEAD = 256
TAIL = 32
BF, F32 = jnp.bfloat16, jnp.float32
MESH = pl.DeviceIdType.MESH


def nt(a, b):
    return lax.dot_general(a, b, (((1,), (1,)), ((), ())), preferred_element_type=F32)


def nn(a, b):
    return lax.dot_general(a, b, (((1,), (0,)), ((), ())), preferred_element_type=F32)


def iota(shape, dim):
    return lax.broadcasted_iota(jnp.int32, shape, dim)


def kernel(
    dims, tok, cot, ids, wts, wg_hbm, wu_hbm, wd_hbm, out, gg_hbm, gu_hbm,
    wgu, wd, wt, picks, sent, got, spread, gath, dx, pair, dxt, pairt, ring_in, ring_out,
    tail_in, tail_out,
    zsum_out, zsum_in, pull, back, home, gbuf, ubuf, lsem, gsend, grecv, zsend, zrecv,
    ysend, yrecv, csend, crecv, psend, precv, rsend, rrecv, wsend, wrecv, hsend, hrecv,
):
    NG, ZH, NY, feat, toks = dims
    rows = feat * 2 * NY
    g = lax.axis_index("group")
    s = lax.axis_index("shard")
    c = lax.rem(s, 2)
    y = lax.rem(lax.div(s, 2), NY)
    z = lax.div(s, 2 * NY)

    def shard_id(zz, yy, cc):
        return (zz * NY + yy) * 2 + cc

    def wrap(v, n):
        return lax.rem(v + 2 * n, n)

    other = shard_id(z, y, 1 - c)
    right = shard_id(z, wrap(y + 1, NY), c)
    left = shard_id(z, wrap(y - 1, NY), c)

    barrier = pltpu.get_barrier_semaphore()

    def greet(gg, ss):
        pl.semaphore_signal(barrier, inc=1, device_id={"group": gg, "shard": ss}, device_id_type=MESH)

    for k in range(1, NG):
        greet(wrap(g + k, NG), s)
    for k in range(1, ZH):
        greet(g, shard_id(wrap(z + k, ZH), y, c))
    greet(g, right)
    greet(g, left)
    greet(g, other)

    loads = [
        pltpu.make_async_copy(wg_hbm.at[0], wgu.at[:, 0:LANES], lsem.at[0]),
        pltpu.make_async_copy(wu_hbm.at[0], wgu.at[:, LANES : 2 * LANES], lsem.at[1]),
    ]
    for q in range(ZH):
        loads.append(pltpu.make_async_copy(wd_hbm.at[0, :, q * rows : (q + 1) * rows], wd.at[q], lsem.at[4 + q]))
    for copy in loads:
        copy.start()

    def send(src, dst, ssem, rsem, gg, ss):
        copy = pltpu.make_async_remote_copy(
            src_ref=src, dst_ref=dst, send_sem=ssem, recv_sem=rsem,
            device_id={"group": gg, "shard": ss}, device_id_type=MESH,
        )
        copy.start()
        pending.append(copy)

    def arrived(dst, ssem, rsem, gg, ss):
        pltpu.make_async_remote_copy(
            src_ref=dst, dst_ref=dst, send_sem=ssem, recv_sem=rsem,
            device_id={"group": gg, "shard": ss}, device_id_type=MESH,
        ).wait_recv()

    pending = []

    who = iota((16, toks), 0)
    first, second = ids[0:1, :] == who, ids[1:2, :] == who
    hit = jnp.where(first, 1, 0) + jnp.where(second, 1, 0)
    upto = jnp.where(iota((toks, toks), 0) <= iota((toks, toks), 1), 1.0, 0.0).astype(BF)
    rank = nn(hit.astype(F32).astype(BF), upto).astype(jnp.int32) - 1
    rank = jnp.where((hit == 1) & (rank < CAP), rank, -1000)
    scale = jnp.where(first, wts[0:1, :], 0.0) + jnp.where(second, wts[1:2, :], 0.0)
    slot = iota((LANES, toks), 0)
    tok_b = tok[...]
    cot_f = cot[...].astype(F32)
    for e in range(NG):
        pick = jnp.where(slot == rank[e : e + 1, :], 1.0, 0.0).astype(BF)
        pick_cot = jnp.where(slot == rank[e : e + 1, :] + CAP, 1.0, 0.0).astype(BF)
        scaled = (cot_f * scale[e : e + 1, :]).astype(BF)
        picks[e] = pick
        sent[e] = (nt(tok_b, pick) + nt(scaled, pick_cot)).astype(BF)

    pl.semaphore_wait(barrier, (NG - 1) + (ZH - 1) + 3)

    for k in range(1, NG):
        e = wrap(g + k, NG)
        send(sent.at[e], got.at[g], gsend.at[k], grecv.at[NG - k], e, s)

    lane = iota((LANES, 1), 0)
    for e in range(NG):
        j = lane + CAP * e
        jc = j - CAP
        to = jnp.where(lane < CAP, j, jnp.where(jc < 256, jc + TOK_LANES, jc + 32))
        to = jnp.where(lane < 2 * CAP, to, -1)
        spread[e] = jnp.where(iota((LANES, ALL_LANES), 1) == to, 1.0, 0.0).astype(BF)
    got[g] = sent[g]
    for copy in loads:
        copy.wait()
    eye = jnp.where(iota((2 * LANES, 2 * LANES), 0) == iota((2 * LANES, 2 * LANES), 1), 1.0, 0.0).astype(BF)
    for q in range(ZH):
        wt[q] = nt(eye, wgu[q * rows : (q + 1) * rows, :]).astype(BF)
    for k in range(1, NG):
        e = wrap(g - k, NG)
        arrived(got.at[e], gsend.at[k], grecv.at[k], e, s)
    block = nn(got[0], spread[0])
    for e in range(1, NG):
        block = block + nn(got[e], spread[e])
    mine = pl.multiple_of(s * feat, 16)
    gath[pl.ds(mine, feat), :] = block.astype(BF)

    def place(zz, yy, cc):
        return gath.at[pl.ds(pl.multiple_of(shard_id(zz, yy, cc) * feat, 16), feat), :]

    reach = [[NY // 2, NY - 1 - NY // 2] if k % 2 == 0 else [NY - 1 - NY // 2, NY // 2] for k in range(ZH)]

    def pass_on(k, direction, t):
        step = 1 if direction == 0 else -1
        if t < reach[k][direction]:
            at = place(wrap(z + k, ZH), wrap(y - step * t, NY), c)
            send(at, at, ysend.at[k, direction, t], yrecv.at[k, direction, t], g, right if direction == 0 else left)

    def across(k, j):
        at = place(wrap(z + k, ZH), wrap(y + j, NY), c)
        send(at, at, csend.at[k, j], crecv.at[k, j], g, other)

    pass_on(0, 0, 0)
    pass_on(0, 1, 0)
    at = place(z, y, c)
    for k in range(1, ZH):
        to = shard_id(wrap(z + k, ZH), y, c)
        send(at, at, zsend.at[k], zrecv.at[ZH - k], g, to)
    across(0, 0)

    order = [0] + [k for k in (1, ZH - 1) if 0 < k < ZH] + [2]
    order = list(dict.fromkeys(k for k in order if k < ZH))
    lag = {k: 0 if k == 0 else 1 for k in order}
    far = max(max(r) for r in reach)
    def hidden(k, pre, hid):
        for j in range(NY):
            arrived(place(wrap(z + k, ZH), wrap(y + j, NY), 1 - c), csend.at[k, j], crecv.at[k, j], g, other)
        q = wrap(z + k, ZH)
        r = pl.ds(pl.multiple_of(q * rows, 16), rows)
        return pre + nn(wt[q], gath[r, 0:TOK_LANES]), hid + nn(wd[q], gath[r, 256:ALL_LANES])

    pre = jnp.zeros((2 * LANES, TOK_LANES), F32)
    hid = jnp.zeros((LANES, TOK_LANES), F32)
    for wave in range(1, far + 2):
        if wave == far + 1:
            pre, hid = hidden(0, pre, hid)
        for k in order:
            t = wave - lag[k]
            if t == 0 and k > 0:
                src = shard_id(wrap(z + k, ZH), y, c)
                arrived(place(wrap(z + k, ZH), y, c), zsend.at[k], zrecv.at[k], g, src)
                pass_on(k, 0, 0)
                pass_on(k, 1, 0)
                across(k, 0)
            for direction in (0, 1):
                step = 1 if direction == 0 else -1
                if 1 <= t <= reach[k][direction]:
                    at = place(wrap(z + k, ZH), wrap(y - step * t, NY), c)
                    arrived(at, ysend.at[k, direction, t - 1], yrecv.at[k, direction, t - 1], g, left if direction == 0 else right)
                    pass_on(k, direction, t)
                    across(k, (-step * t) % NY)
    for k in order[1:]:
        pre, hid = hidden(k, pre, hid)
    hid = jnp.concatenate([hid[:, 128:384], pltpu.roll(hid[:, 0:128], 96, 1)], axis=1)
    gate_pre, up_value = pre[0:LANES, :], pre[LANES : 2 * LANES, :]
    sig = 1.0 / (1.0 + jnp.exp(-gate_pre))
    live = iota((LANES, TOK_LANES), 1) < NG * CAP
    gate_grad = jnp.where(live, hid * up_value * sig * (1.0 + gate_pre * (1.0 - sig)), 0.0).astype(BF)
    up_grad = jnp.where(live, hid * gate_pre * sig, 0.0).astype(BF)
    grads = jnp.concatenate([gate_grad, up_grad], axis=0)

    def inputs(k):
        q = wrap(z + k, ZH)
        r = pl.ds(pl.multiple_of(q * rows, 16), rows)
        v = nn(wgu[r, :], grads[:, 0:HEAD]).astype(BF)
        for m in range(NY):
            for cc in range(2):
                dx[cc, q * NY + m] = v[(2 * m + cc) * feat : (2 * m + cc + 1) * feat, :]
        here = pl.ds(q * NY, NY)
        send(dx.at[1 - c, here], pair.at[here], psend.at[k], precv.at[k], g, other)

    def tails():
        last = grads[:, HEAD:TOK_LANES].astype(F32)
        v = nn(wgu[0:rows, :], last.astype(BF))
        for q in range(1, ZH):
            v = v + nn(wgu[q * rows : (q + 1) * rows, :], pltpu.roll(last, TAIL * q, 1).astype(BF))
        v = v.astype(BF)
        for m in range(NY):
            for cc in range(2):
                dxt[cc, m] = v[(2 * m + cc) * feat : (2 * m + cc + 1) * feat, :]
        send(dxt.at[1 - c], pairt, psend.at[ZH], precv.at[ZH], g, other)

    def paired(k):
        here = pl.ds(wrap(z + k, ZH) * NY, NY)
        at = pairt if k == ZH else pair.at[here]
        arrived(at, psend.at[k], precv.at[k], g, other)

    def own(k, yy):
        if k == ZH:
            return dxt[c, yy].astype(F32) + pairt[yy].astype(F32)
        at = wrap(z + k, ZH) * NY + yy
        return dx[c, at].astype(F32) + pair[at].astype(F32)

    stores = []

    def weight_grads(i):
        r = slice(i * tall, (i + 1) * tall)
        v = nt(gath[r, 0:TOK_LANES], grads).astype(BF)
        gbuf[r, :] = v[:, 0:LANES]
        ubuf[r, :] = v[:, LANES : 2 * LANES]

    finish = [k for k in order if k][::-1] + [0]
    finish = finish[:1] + [ZH] + finish[1:]
    reach.append(reach[0])

    def ring(k, t):
        for direction in (0, 1):
            step = 1 if direction == 0 else -1
            length = reach[k][direction]
            if t > length:
                continue
            v = own(k, wrap(y + step * (length - t + 1), NY))
            into, outof = (tail_in, tail_out) if k == ZH else (ring_in.at[k], ring_out.at[k])
            if t > 1:
                at = into.at[direction, t - 2]
                arrived(at, rsend.at[k, direction, t - 2], rrecv.at[k, direction, t - 2], g, left if direction == 0 else right)
                v = v + at[...].astype(F32)
            outof[direction, t - 1] = v.astype(BF)
            send(
                outof.at[direction, t - 1], into.at[direction, t - 1],
                rsend.at[k, direction, t - 1], rrecv.at[k, direction, t - 1],
                g, right if direction == 0 else left,
            )

    for i, k in enumerate(finish):
        if k == ZH:
            tails()
        else:
            inputs(k)
        if i:
            paired(finish[i - 1])
            ring(finish[i - 1], 1)
    paired(finish[-1])
    ring(finish[-1], 1)
    pieces = 2 * ZH
    tall = rows // 2
    done = 0
    for t in range(2, far + 1):
        while done < min(pieces, (t - 1) * -(-pieces // (far - 1))):
            weight_grads(done)
            done += 1
        for k in finish:
            ring(k, t)
    for buf, hbm, n in ((gbuf, gg_hbm, 3), (ubuf, gu_hbm, 4)):
        copy = pltpu.make_async_copy(buf, hbm.at[0], lsem.at[n])
        copy.start()
        stores.append(copy)
    for e in range(NG):
        l = iota((TOK_LANES, LANES), 1)
        j = l + CAP * e
        j = jnp.where(j < HEAD, j, j + TAIL * z)
        pull[e] = jnp.where((iota((TOK_LANES, LANES), 0) == j) & (l < CAP), 1.0, 0.0).astype(BF)
    for k in [ZH] + [k for k in finish if k < ZH]:
        v = own(k, y)
        into = tail_in if k == ZH else ring_in.at[k]
        for direction in (0, 1):
            t = reach[k][direction]
            at = into.at[direction, t - 1]
            arrived(at, rsend.at[k, direction, t - 1], rrecv.at[k, direction, t - 1], g, left if direction == 0 else right)
            v = v + at[...].astype(F32)
        if k == ZH:
            tail = v
        elif k:
            zsum_out[k, :, 0:HEAD] = v.astype(BF)
            zsum_out[k, :, HEAD:TOK_LANES] = tail.astype(BF)
            to = shard_id(wrap(z + k, ZH), y, c)
            send(zsum_out.at[k], zsum_in.at[ZH - k], wsend.at[k], wrecv.at[ZH - k], g, to)
        else:
            total = jnp.concatenate([v, tail], axis=1)
    for k in range(1, ZH):
        src = shard_id(wrap(z + k, ZH), y, c)
        arrived(zsum_in.at[k], wsend.at[k], wrecv.at[k], g, src)
        total = total + zsum_in[k].astype(F32)
    total = total.astype(BF)

    for e in range(NG):
        back[e] = nn(total, pull[e]).astype(BF)
    for k in range(1, NG):
        e = wrap(g + k, NG)
        send(back.at[e], home.at[g], hsend.at[k], hrecv.at[NG - k], e, s)
    home[g] = back[g]
    for k in range(1, NG):
        e = wrap(g - k, NG)
        arrived(home.at[e], hsend.at[k], hrecv.at[k], e, s)
    res = nn(home[0], picks[0])
    for e in range(1, NG):
        res = res + nn(home[e], picks[e])
    out[...] = res.astype(BF)

    for copy in pending:
        copy.wait_send()
    for copy in stores:
        copy.wait()


def finish(out_in, gg_in, gu_in, out, gg, gu, sem):
    copies = [
        pltpu.make_async_copy(a, b, sem.at[i])
        for i, (a, b) in enumerate(((out_in, out), (gg_in, gg), (gu_in, gu)))
    ]
    for copy in copies:
        copy.start()
    for copy in copies:
        copy.wait()


def layout(shards):
    ny = 8 if shards == 64 else 4
    return shards // (2 * ny), ny


def body(tokens, cotangent, expert_ids, route_weight, w_gate, w_up, w_down):
    NG, NS = lax.axis_size("group"), lax.axis_size("shard")
    ZH, NY = layout(NS)
    toks, feat = tokens.shape
    depth = NS * feat
    far = NY // 2
    vmem = pl.BlockSpec(memory_space=pltpu.VMEM)
    hbm = pl.BlockSpec(memory_space=pl.ANY)
    far_hbm = pl.BlockSpec(memory_space=pltpu.MemorySpace.HBM)
    dma = pltpu.SemaphoreType.DMA
    half = (ZH * NY, feat, HEAD)
    ring = (ZH, 2, far, feat, HEAD)
    tail = (2, far, feat, LANES)
    out, gg, gu = pl.pallas_call(
        functools.partial(kernel, (NG, ZH, NY, feat, toks)),
        out_shape=(
            jax.ShapeDtypeStruct((feat, toks), BF),
            jax.ShapeDtypeStruct(w_gate.shape, BF),
            jax.ShapeDtypeStruct(w_up.shape, BF),
        ),
        in_specs=[vmem] * 4 + [far_hbm] * 3,
        out_specs=(vmem, hbm, hbm),
        scratch_shapes=[
            pltpu.VMEM((depth, 2 * LANES), BF),
            pltpu.VMEM((ZH, LANES, depth // ZH), BF),
            pltpu.VMEM((ZH, 2 * LANES, depth // ZH), BF),
            pltpu.VMEM((NG, LANES, toks), BF),
            pltpu.VMEM((NG, feat, LANES), BF),
            pltpu.VMEM((NG, feat, LANES), BF),
            pltpu.VMEM((NG, LANES, ALL_LANES), BF),
            pltpu.VMEM((depth, ALL_LANES), BF),
            pltpu.VMEM((2,) + half, BF),
            pltpu.VMEM(half, BF),
            pltpu.VMEM((2, NY, feat, LANES), BF),
            pltpu.VMEM((NY, feat, LANES), BF),
            pltpu.VMEM(ring, BF),
            pltpu.VMEM(ring, BF),
            pltpu.VMEM(tail, BF),
            pltpu.VMEM(tail, BF),
            pltpu.VMEM((ZH, feat, TOK_LANES), BF),
            pltpu.VMEM((ZH, feat, TOK_LANES), BF),
            pltpu.VMEM((NG, TOK_LANES, LANES), BF),
            pltpu.VMEM((NG, feat, LANES), BF),
            pltpu.VMEM((NG, feat, LANES), BF),
            pltpu.VMEM((depth, LANES), BF),
            pltpu.VMEM((depth, LANES), BF),
            dma((4 + ZH,)),
            dma((NG,)), dma((NG,)),
            dma((ZH,)), dma((ZH,)),
            dma((ZH, 2, far)), dma((ZH, 2, far)),
            dma((ZH, NY)), dma((ZH, NY)),
            dma((ZH + 1,)), dma((ZH + 1,)),
            dma((ZH + 1, 2, far)), dma((ZH + 1, 2, far)),
            dma((ZH,)), dma((ZH,)),
            dma((NG,)), dma((NG,)),
        ],
        compiler_params=pltpu.CompilerParams(collective_id=0, has_side_effects=True, vmem_limit_bytes=32 << 20),
        name="moe_backward",
    )(*(
        pltpu.with_memory_space_constraint(a, pltpu.MemorySpace.HBM)
        for a in (tokens.T, cotangent.T, expert_ids.T, route_weight.T, w_gate, w_up, w_down)
    ))
    out, gg, gu = pl.pallas_call(
        finish,
        out_shape=tuple(jax.ShapeDtypeStruct(a.shape, a.dtype) for a in (out, gg, gu)),
        in_specs=[hbm] * 3,
        out_specs=(hbm,) * 3,
        scratch_shapes=[dma((3,))],
        compiler_params=pltpu.CompilerParams(vmem_limit_bytes=4 << 20),
        name="finish",
    )(out, gg, gu)
    return out.T, gg, gu


def solution(mesh):
    in_specs = (
        P("group", "shard"),
        P("group", "shard"),
        P("group", None),
        P("group", None),
        P("group", None, "shard"),
        P("group", None, "shard"),
        P("group", "shard", None),
    )
    out_specs = (P("group", "shard"), P("group", None, "shard"), P("group", None, "shard"))
    return jax.shard_map(body, mesh=mesh, in_specs=in_specs, out_specs=out_specs, check_vma=False)
```

```python
import functools

import jax
import jax.numpy as jnp
from jax import lax
from jax.experimental import pallas as pl
from jax.experimental.pallas import tpu as pltpu
from jax.sharding import PartitionSpec as P

CAP = 36
LANES = 128
TOK_LANES = 384
ALL_LANES = 640
HEAD = 256
TAIL = 32
BF, F32 = jnp.bfloat16, jnp.float32
MESH = pl.DeviceIdType.MESH


def nt(a, b):
    return lax.dot_general(a, b, (((1,), (1,)), ((), ())), preferred_element_type=F32)


def nn(a, b):
    return lax.dot_general(a, b, (((1,), (0,)), ((), ())), preferred_element_type=F32)


def iota(shape, dim):
    return lax.broadcasted_iota(jnp.int32, shape, dim)


def kernel(
    dims, tok_hbm, cot_hbm, ids_hbm, wts_hbm, wg_hbm, wu_hbm, wd_hbm, out, gg_hbm, gu_hbm,
    tok, cot, ids, wts, wgu, wd, wt, picks, sent, got, spread, gath, dx, pair, dxt, pairt, ring_in, ring_out,
    tail_in, tail_out,
    zsum_out, zsum_in, pull, back, home, gbuf, ubuf, isem, lsem, gsend, grecv, zsend, zrecv,
    ysend, yrecv, csend, crecv, psend, precv, rsend, rrecv, wsend, wrecv, hsend, hrecv,
):
    NG, ZH, NY, feat, toks = dims
    rows = feat * 2 * NY
    g = lax.axis_index("group")
    s = lax.axis_index("shard")
    c = lax.rem(s, 2)
    y = lax.rem(lax.div(s, 2), NY)
    z = lax.div(s, 2 * NY)

    def shard_id(zz, yy, cc):
        return (zz * NY + yy) * 2 + cc

    def wrap(v, n):
        return lax.rem(v + 2 * n, n)

    other = shard_id(z, y, 1 - c)
    right = shard_id(z, wrap(y + 1, NY), c)
    left = shard_id(z, wrap(y - 1, NY), c)

    barrier = pltpu.get_barrier_semaphore()

    def greet(gg, ss):
        pl.semaphore_signal(barrier, inc=1, device_id={"group": gg, "shard": ss}, device_id_type=MESH)

    for k in range(1, NG):
        greet(wrap(g + k, NG), s)
    for k in range(1, ZH):
        greet(g, shard_id(wrap(z + k, ZH), y, c))
    greet(g, right)
    greet(g, left)
    greet(g, other)

    small = [
        pltpu.make_async_copy(h, v, isem.at[i])
        for i, (h, v) in enumerate(((ids_hbm, ids), (wts_hbm, wts), (tok_hbm, tok), (cot_hbm, cot)))
    ]
    for copy in small:
        copy.start()
    loads = [
        pltpu.make_async_copy(wg_hbm.at[0], wgu.at[:, 0:LANES], lsem.at[0]),
        pltpu.make_async_copy(wu_hbm.at[0], wgu.at[:, LANES : 2 * LANES], lsem.at[1]),
    ]
    for q in range(ZH):
        loads.append(pltpu.make_async_copy(wd_hbm.at[0, :, q * rows : (q + 1) * rows], wd.at[q], lsem.at[4 + q]))
    for copy in loads:
        copy.start()

    def send(src, dst, ssem, rsem, gg, ss):
        copy = pltpu.make_async_remote_copy(
            src_ref=src, dst_ref=dst, send_sem=ssem, recv_sem=rsem,
            device_id={"group": gg, "shard": ss}, device_id_type=MESH,
        )
        copy.start()
        pending.append(copy)

    def arrived(dst, ssem, rsem, gg, ss):
        pltpu.make_async_remote_copy(
            src_ref=dst, dst_ref=dst, send_sem=ssem, recv_sem=rsem,
            device_id={"group": gg, "shard": ss}, device_id_type=MESH,
        ).wait_recv()

    pending = []

    for copy in small:
        copy.wait()

    who = iota((16, toks), 0)
    first, second = ids[0:1, :] == who, ids[1:2, :] == who
    hit = jnp.where(first, 1, 0) + jnp.where(second, 1, 0)
    upto = jnp.where(iota((toks, toks), 0) <= iota((toks, toks), 1), 1.0, 0.0).astype(BF)
    rank = nn(hit.astype(F32).astype(BF), upto).astype(jnp.int32) - 1
    rank = jnp.where((hit == 1) & (rank < CAP), rank, -1000)
    scale = jnp.where(first, wts[0:1, :], 0.0) + jnp.where(second, wts[1:2, :], 0.0)
    slot = iota((LANES, toks), 0)
    tok_b = tok[...]
    cot_f = cot[...].astype(F32)
    for e in range(NG):
        pick = jnp.where(slot == rank[e : e + 1, :], 1.0, 0.0).astype(BF)
        pick_cot = jnp.where(slot == rank[e : e + 1, :] + CAP, 1.0, 0.0).astype(BF)
        scaled = (cot_f * scale[e : e + 1, :]).astype(BF)
        picks[e] = pick
        sent[e] = (nt(tok_b, pick) + nt(scaled, pick_cot)).astype(BF)

    pl.semaphore_wait(barrier, (NG - 1) + (ZH - 1) + 3)

    for k in range(1, NG):
        e = wrap(g + k, NG)
        send(sent.at[e], got.at[g], gsend.at[k], grecv.at[NG - k], e, s)

    lane = iota((LANES, 1), 0)
    for e in range(NG):
        j = lane + CAP * e
        jc = j - CAP
        to = jnp.where(lane < CAP, j, jnp.where(jc < 256, jc + TOK_LANES, jc + 32))
        to = jnp.where(lane < 2 * CAP, to, -1)
        spread[e] = jnp.where(iota((LANES, ALL_LANES), 1) == to, 1.0, 0.0).astype(BF)
    got[g] = sent[g]
    for copy in loads:
        copy.wait()
    eye = jnp.where(iota((2 * LANES, 2 * LANES), 0) == iota((2 * LANES, 2 * LANES), 1), 1.0, 0.0).astype(BF)
    for q in range(ZH):
        wt[q] = nt(eye, wgu[q * rows : (q + 1) * rows, :]).astype(BF)
    for k in range(1, NG):
        e = wrap(g - k, NG)
        arrived(got.at[e], gsend.at[k], grecv.at[k], e, s)
    block = nn(got[0], spread[0])
    for e in range(1, NG):
        block = block + nn(got[e], spread[e])
    gath[z, y, c] = block.astype(BF)

    def place(zz, yy, cc):
        return gath.at[zz, yy, cc]

    reach = [[NY // 2, NY - 1 - NY // 2] if k % 2 == 0 else [NY - 1 - NY // 2, NY // 2] for k in range(ZH)]

    def pass_on(k, direction, t):
        step = 1 if direction == 0 else -1
        if t < reach[k][direction]:
            at = place(wrap(z + k, ZH), wrap(y - step * t, NY), c)
            send(at, at, ysend.at[k, direction, t], yrecv.at[k, direction, t], g, right if direction == 0 else left)

    def across(k):
        at = gath.at[wrap(z + k, ZH), :, c]
        send(at, at, csend.at[k], crecv.at[k], g, other)

    pass_on(0, 0, 0)
    pass_on(0, 1, 0)
    at = place(z, y, c)
    for k in range(1, ZH):
        to = shard_id(wrap(z + k, ZH), y, c)
        send(at, at, zsend.at[k], zrecv.at[ZH - k], g, to)

    order = [0] + [k for k in (1, ZH - 1) if 0 < k < ZH] + [2]
    order = list(dict.fromkeys(k for k in order if k < ZH))
    lag = {k: 0 if k == 0 else 1 for k in order}
    far = max(max(r) for r in reach)
    def hidden(k, pre, hid):
        q = wrap(z + k, ZH)
        arrived(gath.at[q, :, 1 - c], csend.at[k], crecv.at[k], g, other)
        return pre + nn(wt[q], gath[q, :, :, :, 0:TOK_LANES].reshape(rows, TOK_LANES)), hid + nn(
            wd[q], gath[q, :, :, :, HEAD:ALL_LANES].reshape(rows, ALL_LANES - HEAD)
        )

    pre = jnp.zeros((2 * LANES, TOK_LANES), F32)
    hid = jnp.zeros((LANES, TOK_LANES), F32)
    for wave in range(1, far + 2):
        if wave == far + 1:
            pre, hid = hidden(0, pre, hid)
        for k in order if wave == 1 else order[1:] + order[:1]:
            t = wave - lag[k]
            if t == 0 and k > 0:
                src = shard_id(wrap(z + k, ZH), y, c)
                arrived(place(wrap(z + k, ZH), y, c), zsend.at[k], zrecv.at[k], g, src)
                pass_on(k, 0, 0)
                pass_on(k, 1, 0)
            for direction in (0, 1) if t >= 0 else ():
                step = 1 if direction == 0 else -1
                if 1 <= t <= reach[k][direction]:
                    at = place(wrap(z + k, ZH), wrap(y - step * t, NY), c)
                    arrived(at, ysend.at[k, direction, t - 1], yrecv.at[k, direction, t - 1], g, left if direction == 0 else right)
                    pass_on(k, direction, t)
            if t == far:
                across(k)
    for k in order[1:]:
        pre, hid = hidden(k, pre, hid)
    hid = jnp.concatenate([hid[:, 128:384], pltpu.roll(hid[:, 0:128], 96, 1)], axis=1)
    gate_pre, up_value = pre[0:LANES, :], pre[LANES : 2 * LANES, :]
    sig = 1.0 / (1.0 + jnp.exp(-gate_pre))
    live = iota((LANES, TOK_LANES), 1) < NG * CAP
    gate_grad = jnp.where(live, hid * up_value * sig * (1.0 + gate_pre * (1.0 - sig)), 0.0).astype(BF)
    up_grad = jnp.where(live, hid * gate_pre * sig, 0.0).astype(BF)
    grads = jnp.concatenate([gate_grad, up_grad], axis=0)

    def inputs(k):
        q = wrap(z + k, ZH)
        r = pl.ds(pl.multiple_of(q * rows, 16), rows)
        v = nn(wgu[r, :], grads[:, 0:HEAD]).astype(BF)
        for m in range(NY):
            for cc in range(2):
                dx[cc, q * NY + m] = v[(2 * m + cc) * feat : (2 * m + cc + 1) * feat, :]
        here = pl.ds(q * NY, NY)
        send(dx.at[1 - c, here], pair.at[here], psend.at[k], precv.at[k], g, other)

    def tails():
        last = grads[:, HEAD:TOK_LANES].astype(F32)
        v = nn(wgu[0:rows, :], last.astype(BF))
        for q in range(1, ZH):
            v = v + nn(wgu[q * rows : (q + 1) * rows, :], pltpu.roll(last, TAIL * q, 1).astype(BF))
        v = v.astype(BF)
        for m in range(NY):
            for cc in range(2):
                dxt[cc, m] = v[(2 * m + cc) * feat : (2 * m + cc + 1) * feat, :]
        send(dxt.at[1 - c], pairt, psend.at[ZH], precv.at[ZH], g, other)

    def paired(k):
        here = pl.ds(wrap(z + k, ZH) * NY, NY)
        at = pairt if k == ZH else pair.at[here]
        arrived(at, psend.at[k], precv.at[k], g, other)

    def own(k, yy):
        if k == ZH:
            return dxt[c, yy].astype(F32) + pairt[yy].astype(F32)
        at = wrap(z + k, ZH) * NY + yy
        return dx[c, at].astype(F32) + pair[at].astype(F32)

    stores = []

    def weight_grads(i):
        r = slice(i * tall, (i + 1) * tall)
        half = pl.ds((i % 2) * (NY // 2), NY // 2)
        v = nt(gath[i // 2, half, :, :, 0:TOK_LANES].reshape(tall, TOK_LANES), grads).astype(BF)
        gbuf[r, :] = v[:, 0:LANES]
        ubuf[r, :] = v[:, LANES : 2 * LANES]

    finish = [k for k in order if k][::-1] + [0]
    finish = finish[:1] + [ZH] + finish[1:]
    reach.append(reach[0])

    def ring(k, t):
        for direction in (0, 1):
            step = 1 if direction == 0 else -1
            length = reach[k][direction]
            if t > length:
                continue
            v = own(k, wrap(y + step * (length - t + 1), NY))
            into, outof = (tail_in, tail_out) if k == ZH else (ring_in.at[k], ring_out.at[k])
            if t > 1:
                at = into.at[direction, t - 2]
                arrived(at, rsend.at[k, direction, t - 2], rrecv.at[k, direction, t - 2], g, left if direction == 0 else right)
                v = v + at[...].astype(F32)
            outof[direction, t - 1] = v.astype(BF)
            send(
                outof.at[direction, t - 1], into.at[direction, t - 1],
                rsend.at[k, direction, t - 1], rrecv.at[k, direction, t - 1],
                g, right if direction == 0 else left,
            )

    for i, k in enumerate(finish):
        if k == ZH:
            tails()
        else:
            inputs(k)
        if i:
            paired(finish[i - 1])
            ring(finish[i - 1], 1)
    paired(finish[-1])
    ring(finish[-1], 1)
    pieces = 2 * ZH
    tall = rows // 2
    done = 0
    for t in range(2, far + 1):
        while done < min(pieces, (t - 1) * -(-pieces // (far - 1))):
            weight_grads(done)
            done += 1
        for k in finish:
            ring(k, t)
    for buf, hbm, n in ((gbuf, gg_hbm, 3), (ubuf, gu_hbm, 4)):
        copy = pltpu.make_async_copy(buf, hbm.at[0], lsem.at[n])
        copy.start()
        stores.append(copy)
    for e in range(NG):
        l = iota((TOK_LANES, LANES), 1)
        j = l + CAP * e
        j = jnp.where(j < HEAD, j, j + TAIL * z)
        pull[e] = jnp.where((iota((TOK_LANES, LANES), 0) == j) & (l < CAP), 1.0, 0.0).astype(BF)
    for k in [ZH] + [k for k in finish if k < ZH]:
        v = own(k, y)
        into = tail_in if k == ZH else ring_in.at[k]
        for direction in (0, 1):
            t = reach[k][direction]
            at = into.at[direction, t - 1]
            arrived(at, rsend.at[k, direction, t - 1], rrecv.at[k, direction, t - 1], g, left if direction == 0 else right)
            v = v + at[...].astype(F32)
        if k == ZH:
            tail = v
        elif k:
            zsum_out[k, :, 0:HEAD] = v.astype(BF)
            zsum_out[k, :, HEAD:TOK_LANES] = tail.astype(BF)
            to = shard_id(wrap(z + k, ZH), y, c)
            send(zsum_out.at[k], zsum_in.at[ZH - k], wsend.at[k], wrecv.at[ZH - k], g, to)
        else:
            total = jnp.concatenate([v, tail], axis=1)
    for k in range(1, ZH):
        src = shard_id(wrap(z + k, ZH), y, c)
        arrived(zsum_in.at[k], wsend.at[k], wrecv.at[k], g, src)
        total = total + zsum_in[k].astype(F32)
    total = total.astype(BF)

    for e in range(NG):
        back[e] = nn(total, pull[e]).astype(BF)
    for k in range(1, NG):
        e = wrap(g + k, NG)
        send(back.at[e], home.at[g], hsend.at[k], hrecv.at[NG - k], e, s)
    home[g] = back[g]
    for k in range(1, NG):
        e = wrap(g - k, NG)
        arrived(home.at[e], hsend.at[k], hrecv.at[k], e, s)
    res = nn(home[0], picks[0])
    for e in range(1, NG):
        res = res + nn(home[e], picks[e])
    out[...] = res.astype(BF)

    for copy in pending:
        copy.wait_send()
    for copy in stores:
        copy.wait()


def finish(out_in, gg_in, gu_in, out, gg, gu, sem):
    copies = [
        pltpu.make_async_copy(a, b, sem.at[i])
        for i, (a, b) in enumerate(((out_in, out), (gg_in, gg), (gu_in, gu)))
    ]
    for copy in copies:
        copy.start()
    for copy in copies:
        copy.wait()


def layout(shards):
    ny = 8 if shards == 64 else 4
    return shards // (2 * ny), ny


def body(tokens, cotangent, expert_ids, route_weight, w_gate, w_up, w_down):
    NG, NS = lax.axis_size("group"), lax.axis_size("shard")
    ZH, NY = layout(NS)
    toks, feat = tokens.shape
    depth = NS * feat
    far = NY // 2
    vmem = pl.BlockSpec(memory_space=pltpu.VMEM)
    hbm = pl.BlockSpec(memory_space=pl.ANY)
    far_hbm = pl.BlockSpec(memory_space=pltpu.MemorySpace.HBM)
    dma = pltpu.SemaphoreType.DMA
    half = (ZH * NY, feat, HEAD)
    ring = (ZH, 2, far, feat, HEAD)
    tail = (2, far, feat, LANES)
    out, gg, gu = pl.pallas_call(
        functools.partial(kernel, (NG, ZH, NY, feat, toks)),
        out_shape=(
            jax.ShapeDtypeStruct((feat, toks), BF),
            jax.ShapeDtypeStruct(w_gate.shape, BF),
            jax.ShapeDtypeStruct(w_up.shape, BF),
        ),
        in_specs=[far_hbm] * 7,
        out_specs=(vmem, hbm, hbm),
        scratch_shapes=[
            pltpu.VMEM((feat, toks), BF),
            pltpu.VMEM((feat, toks), BF),
            pltpu.VMEM((expert_ids.shape[1], toks), jnp.int32),
            pltpu.VMEM((route_weight.shape[1], toks), F32),
            pltpu.VMEM((depth, 2 * LANES), BF),
            pltpu.VMEM((ZH, LANES, depth // ZH), BF),
            pltpu.VMEM((ZH, 2 * LANES, depth // ZH), BF),
            pltpu.VMEM((NG, LANES, toks), BF),
            pltpu.VMEM((NG, feat, LANES), BF),
            pltpu.VMEM((NG, feat, LANES), BF),
            pltpu.VMEM((NG, LANES, ALL_LANES), BF),
            pltpu.VMEM((ZH, NY, 2, feat, ALL_LANES), BF),
            pltpu.VMEM((2,) + half, BF),
            pltpu.VMEM(half, BF),
            pltpu.VMEM((2, NY, feat, LANES), BF),
            pltpu.VMEM((NY, feat, LANES), BF),
            pltpu.VMEM(ring, BF),
            pltpu.VMEM(ring, BF),
            pltpu.VMEM(tail, BF),
            pltpu.VMEM(tail, BF),
            pltpu.VMEM((ZH, feat, TOK_LANES), BF),
            pltpu.VMEM((ZH, feat, TOK_LANES), BF),
            pltpu.VMEM((NG, TOK_LANES, LANES), BF),
            pltpu.VMEM((NG, feat, LANES), BF),
            pltpu.VMEM((NG, feat, LANES), BF),
            pltpu.VMEM((depth, LANES), BF),
            pltpu.VMEM((depth, LANES), BF),
            dma((4,)),
            dma((4 + ZH,)),
            dma((NG,)), dma((NG,)),
            dma((ZH,)), dma((ZH,)),
            dma((ZH, 2, far)), dma((ZH, 2, far)),
            dma((ZH,)), dma((ZH,)),
            dma((ZH + 1,)), dma((ZH + 1,)),
            dma((ZH + 1, 2, far)), dma((ZH + 1, 2, far)),
            dma((ZH,)), dma((ZH,)),
            dma((NG,)), dma((NG,)),
        ],
        compiler_params=pltpu.CompilerParams(collective_id=0, has_side_effects=True, vmem_limit_bytes=32 << 20),
        name="moe_backward",
    )(*(
        pltpu.with_memory_space_constraint(a, pltpu.MemorySpace.HBM)
        for a in (tokens.T, cotangent.T, expert_ids.T, route_weight.T, w_gate, w_up, w_down)
    ))
    out, gg, gu = pl.pallas_call(
        finish,
        out_shape=tuple(jax.ShapeDtypeStruct(a.shape, a.dtype) for a in (out, gg, gu)),
        in_specs=[hbm] * 3,
        out_specs=(hbm,) * 3,
        scratch_shapes=[dma((3,))],
        compiler_params=pltpu.CompilerParams(vmem_limit_bytes=4 << 20),
        name="finish",
    )(out, gg, gu)
    return out.T, gg, gu


def solution(mesh):
    in_specs = (
        P("group", "shard"),
        P("group", "shard"),
        P("group", None),
        P("group", None),
        P("group", None, "shard"),
        P("group", None, "shard"),
        P("group", "shard", None),
    )
    out_specs = (P("group", "shard"), P("group", None, "shard"), P("group", None, "shard"))
    return jax.shard_map(body, mesh=mesh, in_specs=in_specs, out_specs=out_specs, check_vma=False)
```

```python
import functools

import jax
import jax.numpy as jnp
from jax import lax
from jax.experimental import pallas as pl
from jax.experimental.pallas import tpu as pltpu
from jax.sharding import PartitionSpec as P

CAP = 36
LANES = 128
TOK_LANES = 384
ALL_LANES = 640
HEAD = 256
TAIL = 32
BF, F32 = jnp.bfloat16, jnp.float32
MESH = pl.DeviceIdType.MESH


def nt(a, b):
    return lax.dot_general(a, b, (((1,), (1,)), ((), ())), preferred_element_type=F32)


def nn(a, b):
    return lax.dot_general(a, b, (((1,), (0,)), ((), ())), preferred_element_type=F32)


def iota(shape, dim):
    return lax.broadcasted_iota(jnp.int32, shape, dim)


def kernel(
    dims, tok_hbm, cot_hbm, ids_hbm, wts_hbm, wg_hbm, wu_hbm, wd_hbm, out, gg_hbm, gu_hbm,
    tok, cot, ids, wts, wgu, wd, wt, picks, sent, got, spread, gath, dx, pair, dxt, pairt, ring_in, ring_out,
    tail_in, tail_out,
    zsum_out, zsum_in, pull, back, home, gbuf, ubuf, isem, lsem, gsend, grecv, zsend, zrecv,
    ysend, yrecv, csend, crecv, psend, precv, rsend, rrecv, wsend, wrecv, hsend, hrecv,
):
    NG, ZH, NY, feat, toks = dims
    rows = feat * 2 * NY
    g = lax.axis_index("group")
    s = lax.axis_index("shard")
    c = lax.rem(s, 2)
    y = lax.rem(lax.div(s, 2), NY)
    z = lax.div(s, 2 * NY)

    def shard_id(zz, yy, cc):
        return (zz * NY + yy) * 2 + cc

    def wrap(v, n):
        return lax.rem(v + 2 * n, n)

    other = shard_id(z, y, 1 - c)
    right = shard_id(z, wrap(y + 1, NY), c)
    left = shard_id(z, wrap(y - 1, NY), c)

    barrier = pltpu.get_barrier_semaphore()

    def greet(gg, ss):
        pl.semaphore_signal(barrier, inc=1, device_id={"group": gg, "shard": ss}, device_id_type=MESH)

    for k in range(1, NG):
        greet(wrap(g + k, NG), s)
    for k in range(1, ZH):
        greet(g, shard_id(wrap(z + k, ZH), y, c))
    greet(g, right)
    greet(g, left)
    greet(g, other)

    small = [
        pltpu.make_async_copy(h, v, isem.at[i])
        for i, (h, v) in enumerate(((ids_hbm, ids), (wts_hbm, wts), (tok_hbm, tok), (cot_hbm, cot)))
    ]
    for copy in small:
        copy.start()
    loads = [
        pltpu.make_async_copy(wg_hbm.at[0], wgu.at[:, 0:LANES], lsem.at[0]),
        pltpu.make_async_copy(wu_hbm.at[0], wgu.at[:, LANES : 2 * LANES], lsem.at[1]),
    ]
    for q in range(ZH):
        loads.append(pltpu.make_async_copy(wd_hbm.at[0, :, q * rows : (q + 1) * rows], wd.at[q], lsem.at[4 + q]))
    for copy in loads:
        copy.start()

    def send(src, dst, ssem, rsem, gg, ss):
        copy = pltpu.make_async_remote_copy(
            src_ref=src, dst_ref=dst, send_sem=ssem, recv_sem=rsem,
            device_id={"group": gg, "shard": ss}, device_id_type=MESH,
        )
        copy.start()
        pending.append(copy)

    def arrived(dst, ssem, rsem, gg, ss):
        pltpu.make_async_remote_copy(
            src_ref=dst, dst_ref=dst, send_sem=ssem, recv_sem=rsem,
            device_id={"group": gg, "shard": ss}, device_id_type=MESH,
        ).wait_recv()

    pending = []

    for copy in small:
        copy.wait()

    who = iota((16, toks), 0)
    first, second = ids[0:1, :] == who, ids[1:2, :] == who
    hit = jnp.where(first, 1, 0) + jnp.where(second, 1, 0)
    upto = jnp.where(iota((toks, toks), 0) <= iota((toks, toks), 1), 1.0, 0.0).astype(BF)
    rank = nn(hit.astype(F32).astype(BF), upto).astype(jnp.int32) - 1
    rank = jnp.where((hit == 1) & (rank < CAP), rank, -1000)
    scale = jnp.where(first, wts[0:1, :], 0.0) + jnp.where(second, wts[1:2, :], 0.0)
    slot = iota((LANES, toks), 0)
    tok_b = tok[...]
    cot_f = cot[...].astype(F32)
    for e in range(NG):
        pick = jnp.where(slot == rank[e : e + 1, :], 1.0, 0.0).astype(BF)
        pick_cot = jnp.where(slot == rank[e : e + 1, :] + CAP, 1.0, 0.0).astype(BF)
        scaled = (cot_f * scale[e : e + 1, :]).astype(BF)
        picks[e] = pick
        sent[e] = (nt(tok_b, pick) + nt(scaled, pick_cot)).astype(BF)

    pl.semaphore_wait(barrier, (NG - 1) + (ZH - 1) + 3)

    for k in range(1, NG):
        e = wrap(g + k, NG)
        send(sent.at[e], got.at[g], gsend.at[k], grecv.at[NG - k], e, s)

    lane = iota((LANES, 1), 0)
    for e in range(NG):
        j = lane + CAP * e
        jc = j - CAP
        to = jnp.where(lane < CAP, j, jnp.where(jc < 256, jc + TOK_LANES, jc + 32))
        to = jnp.where(lane < 2 * CAP, to, -1)
        spread[e] = jnp.where(iota((LANES, ALL_LANES), 1) == to, 1.0, 0.0).astype(BF)
    got[g] = sent[g]
    for copy in loads:
        copy.wait()
    eye = jnp.where(iota((2 * LANES, 2 * LANES), 0) == iota((2 * LANES, 2 * LANES), 1), 1.0, 0.0).astype(BF)
    for q in range(ZH):
        wt[q] = nt(eye, wgu[q * rows : (q + 1) * rows, :]).astype(BF)
    for k in range(1, NG):
        e = wrap(g - k, NG)
        arrived(got.at[e], gsend.at[k], grecv.at[k], e, s)
    block = nn(got[0], spread[0])
    for e in range(1, NG):
        block = block + nn(got[e], spread[e])
    gath[z, y, c] = block.astype(BF)

    def place(zz, yy, cc):
        return gath.at[zz, yy, cc]

    reach = [[NY // 2, NY - 1 - NY // 2] if k % 2 == 0 else [NY - 1 - NY // 2, NY // 2] for k in range(ZH)]

    def pass_on(k, direction, t):
        step = 1 if direction == 0 else -1
        if t < reach[k][direction]:
            at = place(wrap(z + k, ZH), wrap(y - step * t, NY), c)
            send(at, at, ysend.at[k, direction, t], yrecv.at[k, direction, t], g, right if direction == 0 else left)

    def across(k):
        at = gath.at[wrap(z + k, ZH), :, c]
        send(at, at, csend.at[k], crecv.at[k], g, other)

    pass_on(0, 0, 0)
    pass_on(0, 1, 0)
    at = place(z, y, c)
    for k in sorted(range(1, ZH), key=lambda k: -min(k, ZH - k)):
        to = shard_id(wrap(z + k, ZH), y, c)
        send(at, at, zsend.at[k], zrecv.at[ZH - k], g, to)

    order = [0] + [k for k in (1, ZH - 1) if 0 < k < ZH] + [2]
    order = list(dict.fromkeys(k for k in order if k < ZH))
    lag = {k: 0 if k == 0 else 1 for k in order}
    far = max(max(r) for r in reach)
    def hidden(k, pre, hid):
        q = wrap(z + k, ZH)
        arrived(gath.at[q, :, 1 - c], csend.at[k], crecv.at[k], g, other)
        return pre + nn(wt[q], gath[q, :, :, :, 0:TOK_LANES].reshape(rows, TOK_LANES)), hid + nn(
            wd[q], gath[q, :, :, :, HEAD:ALL_LANES].reshape(rows, ALL_LANES - HEAD)
        )

    pre = jnp.zeros((2 * LANES, TOK_LANES), F32)
    hid = jnp.zeros((LANES, TOK_LANES), F32)
    for wave in range(1, far + 2):
        if wave == far + 1:
            pre, hid = hidden(0, pre, hid)
        for k in order if wave == 1 else order[1:] + order[:1]:
            t = wave - lag[k]
            if t == 0 and k > 0:
                src = shard_id(wrap(z + k, ZH), y, c)
                arrived(place(wrap(z + k, ZH), y, c), zsend.at[k], zrecv.at[k], g, src)
                pass_on(k, 0, 0)
                pass_on(k, 1, 0)
            for direction in (0, 1) if t >= 0 else ():
                step = 1 if direction == 0 else -1
                if 1 <= t <= reach[k][direction]:
                    at = place(wrap(z + k, ZH), wrap(y - step * t, NY), c)
                    arrived(at, ysend.at[k, direction, t - 1], yrecv.at[k, direction, t - 1], g, left if direction == 0 else right)
                    pass_on(k, direction, t)
            if t == far:
                across(k)
    for k in order[1:]:
        pre, hid = hidden(k, pre, hid)
    hid = jnp.concatenate([hid[:, 128:384], pltpu.roll(hid[:, 0:128], 96, 1)], axis=1)
    gate_pre, up_value = pre[0:LANES, :], pre[LANES : 2 * LANES, :]
    sig = 1.0 / (1.0 + jnp.exp(-gate_pre))
    live = iota((LANES, TOK_LANES), 1) < NG * CAP
    gate_grad = jnp.where(live, hid * up_value * sig * (1.0 + gate_pre * (1.0 - sig)), 0.0).astype(BF)
    up_grad = jnp.where(live, hid * gate_pre * sig, 0.0).astype(BF)
    grads = jnp.concatenate([gate_grad, up_grad], axis=0)

    def inputs(k):
        q = wrap(z + k, ZH)
        r = pl.ds(pl.multiple_of(q * rows, 16), rows)
        v = nn(wgu[r, :], grads[:, 0:HEAD]).astype(BF)
        for m in range(NY):
            for cc in range(2):
                dx[cc, q * NY + m] = v[(2 * m + cc) * feat : (2 * m + cc + 1) * feat, :]
        here = pl.ds(q * NY, NY)
        send(dx.at[1 - c, here], pair.at[here], psend.at[k], precv.at[k], g, other)

    def tails():
        last = grads[:, HEAD:TOK_LANES].astype(F32)
        v = nn(wgu[0:rows, :], last.astype(BF))
        for q in range(1, ZH):
            v = v + nn(wgu[q * rows : (q + 1) * rows, :], pltpu.roll(last, TAIL * q, 1).astype(BF))
        v = v.astype(BF)
        for m in range(NY):
            for cc in range(2):
                dxt[cc, m] = v[(2 * m + cc) * feat : (2 * m + cc + 1) * feat, :]
        send(dxt.at[1 - c], pairt, psend.at[ZH], precv.at[ZH], g, other)

    def paired(k):
        here = pl.ds(wrap(z + k, ZH) * NY, NY)
        at = pairt if k == ZH else pair.at[here]
        arrived(at, psend.at[k], precv.at[k], g, other)

    def own(k, yy):
        if k == ZH:
            return dxt[c, yy].astype(F32) + pairt[yy].astype(F32)
        at = wrap(z + k, ZH) * NY + yy
        return dx[c, at].astype(F32) + pair[at].astype(F32)

    stores = []

    def weight_grads(i):
        r = slice(i * tall, (i + 1) * tall)
        half = pl.ds((i % 2) * (NY // 2), NY // 2)
        v = nt(gath[i // 2, half, :, :, 0:TOK_LANES].reshape(tall, TOK_LANES), grads).astype(BF)
        gbuf[r, :] = v[:, 0:LANES]
        ubuf[r, :] = v[:, LANES : 2 * LANES]

    finish = [k for k in order if k][::-1] + [0]
    finish = finish[:1] + [ZH] + finish[1:]
    reach.append(reach[0])

    def ring(k, t):
        for direction in (0, 1):
            step = 1 if direction == 0 else -1
            length = reach[k][direction]
            if t > length:
                continue
            v = own(k, wrap(y + step * (length - t + 1), NY))
            into, outof = (tail_in, tail_out) if k == ZH else (ring_in.at[k], ring_out.at[k])
            if t > 1:
                at = into.at[direction, t - 2]
                arrived(at, rsend.at[k, direction, t - 2], rrecv.at[k, direction, t - 2], g, left if direction == 0 else right)
                v = v + at[...].astype(F32)
            outof[direction, t - 1] = v.astype(BF)
            send(
                outof.at[direction, t - 1], into.at[direction, t - 1],
                rsend.at[k, direction, t - 1], rrecv.at[k, direction, t - 1],
                g, right if direction == 0 else left,
            )

    for i, k in enumerate(finish):
        if k == ZH:
            tails()
        else:
            inputs(k)
        if i:
            paired(finish[i - 1])
            ring(finish[i - 1], 1)
    paired(finish[-1])
    ring(finish[-1], 1)
    pieces = 2 * ZH
    tall = rows // 2
    done = 0
    for t in range(2, far + 1):
        while done < min(pieces, (t - 1) * -(-pieces // (far - 1))):
            weight_grads(done)
            done += 1
        for k in finish:
            ring(k, t)
    for buf, hbm, n in ((gbuf, gg_hbm, 3), (ubuf, gu_hbm, 4)):
        copy = pltpu.make_async_copy(buf, hbm.at[0], lsem.at[n])
        copy.start()
        stores.append(copy)
    for e in range(NG):
        l = iota((TOK_LANES, LANES), 1)
        j = l + CAP * e
        j = jnp.where(j < HEAD, j, j + TAIL * z)
        pull[e] = jnp.where((iota((TOK_LANES, LANES), 0) == j) & (l < CAP), 1.0, 0.0).astype(BF)
    for k in [ZH] + [k for k in finish if k < ZH]:
        v = own(k, y)
        into = tail_in if k == ZH else ring_in.at[k]
        for direction in (0, 1):
            t = reach[k][direction]
            at = into.at[direction, t - 1]
            arrived(at, rsend.at[k, direction, t - 1], rrecv.at[k, direction, t - 1], g, left if direction == 0 else right)
            v = v + at[...].astype(F32)
        if k == ZH:
            tail = v
        elif k:
            zsum_out[k, :, 0:HEAD] = v.astype(BF)
            zsum_out[k, :, HEAD:TOK_LANES] = tail.astype(BF)
            to = shard_id(wrap(z + k, ZH), y, c)
            send(zsum_out.at[k], zsum_in.at[ZH - k], wsend.at[k], wrecv.at[ZH - k], g, to)
        else:
            total = jnp.concatenate([v, tail], axis=1)
    for k in range(1, ZH):
        src = shard_id(wrap(z + k, ZH), y, c)
        arrived(zsum_in.at[k], wsend.at[k], wrecv.at[k], g, src)
        total = total + zsum_in[k].astype(F32)
    total = total.astype(BF)

    for e in range(NG):
        back[e] = nn(total, pull[e]).astype(BF)
    for k in range(1, NG):
        e = wrap(g + k, NG)
        send(back.at[e], home.at[g], hsend.at[k], hrecv.at[NG - k], e, s)
    home[g] = back[g]
    for k in range(1, NG):
        e = wrap(g - k, NG)
        arrived(home.at[e], hsend.at[k], hrecv.at[k], e, s)
    res = nn(home[0], picks[0])
    for e in range(1, NG):
        res = res + nn(home[e], picks[e])
    out[...] = res.astype(BF)

    for copy in pending:
        copy.wait_send()
    for copy in stores:
        copy.wait()


def finish(out_in, gg_in, gu_in, out, gg, gu, sem):
    copies = [
        pltpu.make_async_copy(a, b, sem.at[i])
        for i, (a, b) in enumerate(((out_in, out), (gg_in, gg), (gu_in, gu)))
    ]
    for copy in copies:
        copy.start()
    for copy in copies:
        copy.wait()


def layout(shards):
    ny = 8 if shards == 64 else 4
    return shards // (2 * ny), ny


def body(tokens, cotangent, expert_ids, route_weight, w_gate, w_up, w_down):
    NG, NS = lax.axis_size("group"), lax.axis_size("shard")
    ZH, NY = layout(NS)
    toks, feat = tokens.shape
    depth = NS * feat
    far = NY // 2
    vmem = pl.BlockSpec(memory_space=pltpu.VMEM)
    hbm = pl.BlockSpec(memory_space=pl.ANY)
    far_hbm = pl.BlockSpec(memory_space=pltpu.MemorySpace.HBM)
    dma = pltpu.SemaphoreType.DMA
    half = (ZH * NY, feat, HEAD)
    ring = (ZH, 2, far, feat, HEAD)
    tail = (2, far, feat, LANES)
    out, gg, gu = pl.pallas_call(
        functools.partial(kernel, (NG, ZH, NY, feat, toks)),
        out_shape=(
            jax.ShapeDtypeStruct((feat, toks), BF),
            jax.ShapeDtypeStruct(w_gate.shape, BF),
            jax.ShapeDtypeStruct(w_up.shape, BF),
        ),
        in_specs=[far_hbm] * 7,
        out_specs=(vmem, hbm, hbm),
        scratch_shapes=[
            pltpu.VMEM((feat, toks), BF),
            pltpu.VMEM((feat, toks), BF),
            pltpu.VMEM((expert_ids.shape[1], toks), jnp.int32),
            pltpu.VMEM((route_weight.shape[1], toks), F32),
            pltpu.VMEM((depth, 2 * LANES), BF),
            pltpu.VMEM((ZH, LANES, depth // ZH), BF),
            pltpu.VMEM((ZH, 2 * LANES, depth // ZH), BF),
            pltpu.VMEM((NG, LANES, toks), BF),
            pltpu.VMEM((NG, feat, LANES), BF),
            pltpu.VMEM((NG, feat, LANES), BF),
            pltpu.VMEM((NG, LANES, ALL_LANES), BF),
            pltpu.VMEM((ZH, NY, 2, feat, ALL_LANES), BF),
            pltpu.VMEM((2,) + half, BF),
            pltpu.VMEM(half, BF),
            pltpu.VMEM((2, NY, feat, LANES), BF),
            pltpu.VMEM((NY, feat, LANES), BF),
            pltpu.VMEM(ring, BF),
            pltpu.VMEM(ring, BF),
            pltpu.VMEM(tail, BF),
            pltpu.VMEM(tail, BF),
            pltpu.VMEM((ZH, feat, TOK_LANES), BF),
            pltpu.VMEM((ZH, feat, TOK_LANES), BF),
            pltpu.VMEM((NG, TOK_LANES, LANES), BF),
            pltpu.VMEM((NG, feat, LANES), BF),
            pltpu.VMEM((NG, feat, LANES), BF),
            pltpu.VMEM((depth, LANES), BF),
            pltpu.VMEM((depth, LANES), BF),
            dma((4,)),
            dma((4 + ZH,)),
            dma((NG,)), dma((NG,)),
            dma((ZH,)), dma((ZH,)),
            dma((ZH, 2, far)), dma((ZH, 2, far)),
            dma((ZH,)), dma((ZH,)),
            dma((ZH + 1,)), dma((ZH + 1,)),
            dma((ZH + 1, 2, far)), dma((ZH + 1, 2, far)),
            dma((ZH,)), dma((ZH,)),
            dma((NG,)), dma((NG,)),
        ],
        compiler_params=pltpu.CompilerParams(collective_id=0, has_side_effects=True, vmem_limit_bytes=32 << 20),
        name="moe_backward",
    )(*(
        pltpu.with_memory_space_constraint(a, pltpu.MemorySpace.HBM)
        for a in (tokens.T, cotangent.T, expert_ids.T, route_weight.T, w_gate, w_up, w_down)
    ))
    out, gg, gu = pl.pallas_call(
        finish,
        out_shape=tuple(jax.ShapeDtypeStruct(a.shape, a.dtype) for a in (out, gg, gu)),
        in_specs=[hbm] * 3,
        out_specs=(hbm,) * 3,
        scratch_shapes=[dma((3,))],
        compiler_params=pltpu.CompilerParams(vmem_limit_bytes=4 << 20),
        name="finish",
    )(out, gg, gu)
    return out.T, gg, gu


def solution(mesh):
    in_specs = (
        P("group", "shard"),
        P("group", "shard"),
        P("group", None),
        P("group", None),
        P("group", None, "shard"),
        P("group", None, "shard"),
        P("group", "shard", None),
    )
    out_specs = (P("group", "shard"), P("group", None, "shard"), P("group", None, "shard"))
    return jax.shard_map(body, mesh=mesh, in_specs=in_specs, out_specs=out_specs, check_vma=False)
```
